32 devices in a mesh: band: 2 (over y), row: 8 (over z, x), col: 2 (over core).
Axes of the slice: x: 2, y: 2, z: 4, core: 2. Of those that a mesh axis runs over, the one named last changes fastest.
Arguments:
- voltages: bfloat16 [4096, 161792], P(('band', 'row', 'col')), parts along dimension 0, may hold values from -6 to 6
- gains: float32 [4096, 32, 2], P(('band', 'row', 'col')), parts along dimension 0, may hold values from -4 to 4
Outputs:
- visibilities: bfloat16 [64, 2048, 2, 2048], P(('band', 'row'), None, None, 'col'), parts along dimension 0
The draws below stay inside these ranges and needn't reach their ends.
There are 2 independent parts, one for each index of `band`. The reference program is written for one: setup_inputs(seed, part) draws one part's arguments, and reference() takes and returns one part's arrays. A program takes and returns all parts, laid end to end along the dimension named above; each array names one. Nothing has to cross between parts.
All inputs are finite; a program needn't handle non-finite values.
Results may differ from the reference program's by a relative error of at most 0.0075.
Values may be sent and summed in bfloat16 or wider, within the bound.
No kernel may reach another device: no remote copies, remote signals or barrier semaphores. Data moves between devices by JAX's collectives and lax.ppermute only.
A program may use at most 192 MiB of HBM per device.

```python
import math
import jax
import jax.numpy as jnp
from jax import lax

FEEDS = 2048
NFFT = 2048
TAPS = 16
CHANS = 32
SPECTRA = 64
FRAMES = 79
CHAN0 = 256
FEED_DEV = 128
SUB = 1
IBLOCK = 2048


def block_levels(rng, shape, split, least, largest):
    factor_of, own = 1.0, jax.random.fold_in(rng, 6)
    for position, shards_of in split:
        heights = jnp.exp(jax.random.uniform(jax.random.fold_in(own, position), (shards_of,), jnp.float32, least / len(split), largest / len(split)))
        factor_of = factor_of * jnp.repeat(heights, shape[position] // shards_of).reshape([-1 if axis == position else 1 for axis in range(len(shape))])
    return factor_of


def gaussian(key, shape, scale, limit, pieces=(), kind=jnp.bfloat16):
    values = jax.random.normal(key, shape, jnp.float32) * scale
    if len(pieces) > 0:
        values = block_levels(key, shape, pieces, -0.22, 0.18) * values
    return jnp.clip(values, min=-limit, max=limit).astype(kind)


def setup_inputs(seed: int = 0, part: int = 0) -> dict:
    arg_keys = jax.random.split(jax.random.key(seed), 3)
    own_keys = jax.random.split(jax.random.fold_in(arg_keys[2], part), 3)
    voltages = gaussian(own_keys[0], (FEEDS, FRAMES * NFFT), 1.0, 6.0, ((0, 16),))
    gains = gaussian(own_keys[1], (FEEDS, CHANS, 2), 0.8, 4.0, ((0, 16),), jnp.float32)
    return dict(voltages=voltages, gains=gains)


def prototype(taps, length):
    total = taps * length
    index = jnp.arange(total).astype(jnp.float32)
    offset = (index - (total - 1) / 2.0) / length
    window = 0.5 - 0.5 * jnp.cos(2.0 * math.pi * (index + 0.5) / total)
    return (jnp.sinc(offset) * window).reshape(taps, length)


def dft_table(length, chans, first):
    sample = jnp.arange(length).astype(jnp.int32)
    channel = (first + jnp.arange(chans)).astype(jnp.int32)
    phase = (sample[:, None] * channel[None, :]) % length
    angle = phase.astype(jnp.float32) * (2.0 * math.pi / length)
    return jnp.concatenate([jnp.cos(angle), -jnp.sin(angle)], axis=1).astype(jnp.bfloat16)


def reference(voltages, gains):
    window = prototype(TAPS, NFFT)
    table = dft_table(NFFT, CHANS, CHAN0)
    scale = float(NFFT) ** -0.5
    blocks = voltages.reshape(FEEDS // FEED_DEV, FEED_DEV, FRAMES, NFFT)

    def channelize(block):
        total = jnp.zeros((FEED_DEV, SPECTRA, NFFT), jnp.float32)
        for tap in range(TAPS):
            total = total + block[:, tap:tap + SPECTRA, :].astype(jnp.float32) * window[tap]
        filtered = total.astype(jnp.bfloat16)
        raw = jnp.dot(filtered.reshape(FEED_DEV * SPECTRA, NFFT), table, preferred_element_type=jnp.float32) * scale
        return raw.reshape(FEED_DEV, SPECTRA, 2 * CHANS)

    raw = lax.map(channelize, blocks).reshape(FEEDS, SPECTRA, 2 * CHANS)
    real_part = raw[:, :, :CHANS]
    imag_part = raw[:, :, CHANS:]
    gain_re = gains[:, None, :, 0]
    gain_im = gains[:, None, :, 1]
    out_re = gain_re * real_part - gain_im * imag_part
    out_im = gain_re * imag_part + gain_im * real_part
    stacked = jnp.stack([out_re, out_im], axis=0)
    spectra = jnp.transpose(stacked, (3, 1, 0, 2)).reshape(CHANS, FEEDS, 2 * SPECTRA).astype(jnp.bfloat16)

    def correlate(chan_rows):
        turned = jnp.concatenate([-chan_rows[:, SPECTRA:], chan_rows[:, :SPECTRA]], axis=1)
        right = jnp.concatenate([chan_rows, turned], axis=0)
        product = jnp.dot(chan_rows, right.T, preferred_element_type=jnp.float32) / SPECTRA
        return product.astype(jnp.bfloat16).reshape(FEEDS, 2, FEEDS)

    result = lax.map(correlate, spectra)
    return result.reshape(CHANS * SUB, IBLOCK, 2, FEEDS)
```

```python
import math, functools
import jax
import jax.numpy as jnp
from jax import lax
from jax.experimental import pallas as pl
from jax.experimental.pallas import tpu as pltpu
from jax.sharding import PartitionSpec as P

FEEDS = 2048
NFFT = 2048
TAPS = 16
SPECTRA = 64
QUAD = 4
LANES = 128
UBLOCK = 17


def prototype(taps, length):
    total = taps * length
    index = jnp.arange(total).astype(jnp.float32)
    offset = (index - (total - 1) / 2.0) / length
    window = 0.5 - 0.5 * jnp.cos(2.0 * math.pi * (index + 0.5) / total)
    return (jnp.sinc(offset) * window).reshape(taps, length)


def dft_table(length, chans, first):
    sample = jnp.arange(length)
    channel = first + jnp.arange(chans)
    phase = sample[:, None] * channel[None, :] % length
    angle = phase.astype(jnp.float32) * (2.0 * math.pi / length)
    return jnp.concatenate([jnp.cos(angle), -jnp.sin(angle)], axis=1).astype(jnp.bfloat16)


def weights_kernel(h_ref, e_ref, o_ref, *, chans):
    wide = 2 * chans
    h = h_ref[...]
    hi = h.astype(jnp.bfloat16).astype(jnp.float32)
    mid = (h - hi).astype(jnp.bfloat16).astype(jnp.float32)
    low = h - hi - mid
    rest = jnp.zeros((LANES - 3 * TAPS, NFFT), jnp.float32)
    parts = jnp.concatenate([hi, mid, low, rest], axis=0).T.astype(jnp.bfloat16)
    spread = (lax.broadcasted_iota(jnp.int32, (wide, QUAD * wide), 1) % wide == lax.broadcasted_iota(jnp.int32, (wide, QUAD * wide), 0))
    table = jnp.dot(e_ref[...], spread.astype(jnp.float32).astype(jnp.bfloat16), preferred_element_type=jnp.float32)
    row = lax.broadcasted_iota(jnp.int32, (LANES, QUAD * wide), 0)
    tap = lax.broadcasted_iota(jnp.int32, (LANES, QUAD * wide), 1) // wide
    for p in range(TAPS // QUAD):
        pick = jnp.where(row < 3 * TAPS, (row % TAPS == QUAD * p + tap).astype(jnp.float32), 0.0).astype(jnp.bfloat16)
        window = jnp.dot(parts, pick, preferred_element_type=jnp.float32)
        o_ref[p] = (window * table).astype(jnp.bfloat16)


def weights(chans):
    window = prototype(TAPS, NFFT)
    table = dft_table(NFFT, chans, NFFT // 8)
    return pl.pallas_call(
        functools.partial(weights_kernel, chans=chans),
        out_shape=jax.ShapeDtypeStruct((TAPS // QUAD, NFFT, QUAD * 2 * chans), jnp.bfloat16),
        in_specs=[pl.BlockSpec(memory_space=pltpu.VMEM)] * 2,
        out_specs=pl.BlockSpec(memory_space=pltpu.VMEM),
        compiler_params=pltpu.CompilerParams(vmem_limit_bytes=24 << 20),
        name="weights",
    )(window, table)


def channelize_kernel(v_ref, w_ref, g_ref, o_ref, x, w, acc, r0, r1, st, sem, wsem, *, first, fb, frames, chans):
    groups = TAPS // QUAD
    urange = SPECTRA + QUAD - 1

    def copy(j):
        return pltpu.make_async_copy(
            v_ref.at[pl.ds(first, fb), pl.ds(j * NFFT, NFFT)], x.at[pl.ds(j * fb, fb), :], sem.at[j])

    def wcopy(p):
        return pltpu.make_async_copy(w_ref.at[p], w.at[p], wsem.at[p])
    for p in range(groups):
        wcopy(p).start()
    for j in range(frames):
        copy(j).start()
    scale = float(NFFT) ** -0.5
    gre = g_ref[pl.ds(0, chans, stride=2), :] * scale
    gim = g_ref[pl.ds(1, chans, stride=2), :] * scale
    g1 = jnp.concatenate([gre] * 4, axis=0).T[first:first + fb]
    g2 = jnp.concatenate([-gim, gim, -gim, gim], axis=0).T[first:first + fb]
    for p in range(groups):
        wcopy(p).wait()
    done = 0
    ready = 0
    u0 = 0
    for region in REGIONS:
        last = min(frames, u0 + sum(region) + QUAD * (groups - 1))
        for j in range(done, last):
            copy(j).wait()
        done = last
        upto = max(0, min(SPECTRA, u0 - QUAD + 1))
        spectra_rows(acc, r0, r1, g1, g2, ready, upto, fb)
        ready = upto
        for un in region:
            total = None
            for p in range(groups):
                d = jnp.dot(x[(u0 + QUAD * p) * fb:(u0 + QUAD * p + un) * fb, :], w[p], preferred_element_type=jnp.float32)
                total = d if total is None else total + d
            acc[u0 * fb:(u0 + un) * fb, :] = total
            u0 += un
    spectra_rows(acc, r0, r1, g1, g2, ready, SPECTRA, fb)
    block = lax.broadcasted_iota(jnp.int32, (SPECTRA, LANES), 1) // chans

    def pick(parts):
        return jnp.where(block < 2, jnp.where(block < 1, parts[0], parts[1]), jnp.where(block < 3, parts[2], parts[3]))
    for f in range(0, fb, 4):
        same = [r0[pl.ds(f + b, SPECTRA, stride=fb), :] for b in range(4)]
        swap = [r1[pl.ds(f + b, SPECTRA, stride=fb), :] for b in range(4)]
        top = pick([same[0], swap[1], same[2], swap[3]])
        low = pick([swap[0], same[1], swap[2], same[3]])
        t = jnp.concatenate([top, low], axis=0).T
        for b in range(4):
            st[pl.ds(f + b, chans, stride=fb), :] = t[b * chans:(b + 1) * chans]
    o_ref[...] = st[...].astype(jnp.bfloat16).reshape(o_ref.shape)


CHUNKS = (2, 2)
REGIONS = ((8, 8), (12, 12), (14, 13))


def spectra_rows(acc, r0, r1, g1, g2, lo, hi, fb):
    s = lo
    while s < hi:
        n = min(SBATCH, hi - s)
        lane = lax.broadcasted_iota(jnp.int32, (n * fb, LANES), 1)
        one = acc[s * fb:(s + n + 1) * fb, 0:LANES] + acc[(s + 2) * fb:(s + n + 3) * fb, LANES:2 * LANES]
        c = jnp.where(lane < LANES // 2, one[:n * fb], one[fb:])
        y = c + pltpu.roll(c, LANES // 2, 1)
        sw = pltpu.roll(y, LANES // 4, 1)
        ga = jnp.concatenate([g1] * n, axis=0)
        gb = jnp.concatenate([g2] * n, axis=0)
        r0[s * fb:(s + n) * fb, :] = ga * y + gb * sw
        r1[s * fb:(s + n) * fb, :] = ga * sw - gb * y
        s += n


SBATCH = 8


def channelize(voltages, w, gt, first, fb):
    frames = voltages.shape[1] // NFFT
    chans = gt.shape[0] // 2
    n = SPECTRA + QUAD - 1
    return pl.pallas_call(
        functools.partial(channelize_kernel, first=first, fb=fb, frames=frames, chans=chans),
        out_shape=jax.ShapeDtypeStruct((chans, fb, 2 * SPECTRA), jnp.bfloat16),
        in_specs=[pl.BlockSpec(memory_space=pl.ANY), pl.BlockSpec(memory_space=pl.ANY), pl.BlockSpec(memory_space=pltpu.VMEM)],
        out_specs=pl.BlockSpec(memory_space=pltpu.VMEM),
        scratch_shapes=[
            pltpu.VMEM((frames * fb, NFFT), jnp.bfloat16),
            pltpu.VMEM(w.shape, jnp.bfloat16),
            pltpu.VMEM((n * fb, QUAD * 2 * chans), jnp.float32),
            pltpu.VMEM((SPECTRA * fb, LANES), jnp.float32),
            pltpu.VMEM((SPECTRA * fb, LANES), jnp.float32),
            pltpu.VMEM((chans * fb, LANES), jnp.float32),
            pltpu.SemaphoreType.DMA((frames,)),
            pltpu.SemaphoreType.DMA((TAPS // QUAD,)),
        ],
        compiler_params=pltpu.CompilerParams(vmem_limit_bytes=56 << 20),
        cost_estimate=pl.CostEstimate(flops=2 * n * fb * TAPS // QUAD * NFFT * QUAD * 2 * chans, bytes_accessed=fb * frames * NFFT * 2, transcendentals=0),
        name="channelize",
    )(voltages, w, gt)


IBLOCK = 512
NSPLIT = 4


def correlate_kernel(*refs, nchunk, rows, pairs):
    own, other = refs[:nchunk], refs[nchunk:2 * nchunk]
    o_ref, lf, right, turned, out, sem = refs[2 * nchunk:]
    col = lax.axis_index("col")
    sizes = [ref.shape[1] for ref in own]
    starts = [sum(sizes[:a]) for a in range(nchunk)]
    fd = sum(sizes)
    nblk = FEEDS // IBLOCK
    jblock = right.shape[0]
    jtiles = jblock // LANES
    half = rows * 2 * fd // jblock

    def put(q, blk, slot, jt):
        return pltpu.make_async_copy(
            out.at[slot, jt], o_ref.reshape(pairs, 2 * FEEDS, jblock).at[q, pl.ds(blk * 2 * IBLOCK, 2 * IBLOCK), pl.ds(jt * LANES, LANES)], sem.at[slot, jt])

    def channel(q, _):
        for r in range(rows):
            for a in range(nchunk):
                for which in range(2):
                    piece = (own if which == 0 else other)[a][r * pairs + q].astype(jnp.float32)
                    c = col if which == 0 else 1 - col
                    fb = sizes[a]
                    lane = lax.broadcasted_iota(jnp.int32, (fb, LANES), 1)
                    sign = jnp.where(lane < SPECTRA, 1.0, -1.0) * (1.0 / SPECTRA)
                    base = pl.multiple_of((r * 2 * fd + c * fd + starts[a]) * 2, LANES // 4)
                    lf[pl.ds(base, fb, stride=2), :] = piece * (1.0 / SPECTRA)
                    lf[pl.ds(base + 1, fb, stride=2), :] = pltpu.roll(piece, SPECTRA, 1) * sign
        for r in range(rows // half):
            for a in range(nchunk):
                for which in range(2):
                    c = col if which == 0 else 1 - col
                    piece = (own if which == 0 else other)[a][(col * (rows // half) + r) * pairs + q]
                    base = pl.multiple_of(r * 2 * fd + c * fd + starts[a], LANES // 8)
                    right[pl.ds(base, sizes[a]), :] = piece
        turned[...] = right[...].T

        def block(blk, _):
            step = q * nblk + blk
            slot = lax.rem(step, 2)

            @pl.when(step >= 2)
            def _():
                for jt in range(jtiles):
                    put(0, 0, slot, jt).wait()
            start = pl.multiple_of(blk * 2 * IBLOCK, 2 * IBLOCK)
            rowsb = lf[pl.ds(start, 2 * IBLOCK), :].astype(jnp.bfloat16)
            width = jblock // NSPLIT
            for k in range(NSPLIT):
                prod = jnp.dot(rowsb, turned[:, k * width:(k + 1) * width], preferred_element_type=jnp.float32).astype(jnp.bfloat16)
                for jt in range(width // LANES):
                    out[slot, k * (width // LANES) + jt] = prod[:, jt * LANES:(jt + 1) * LANES]
                    put(q, blk, slot, k * (width // LANES) + jt).start()
            return 0
        lax.fori_loop(0, nblk, block, 0)
        return 0
    lax.fori_loop(0, pairs, channel, 0)
    for slot in range(2):
        for jt in range(jtiles):
            put(0, 0, slot, jt).wait()


def correlate(own, other, rows, pairs):
    nchunk = len(own)
    jblock = FEEDS // 2
    return pl.pallas_call(
        functools.partial(correlate_kernel, nchunk=nchunk, rows=rows, pairs=pairs),
        out_shape=jax.ShapeDtypeStruct((pairs, FEEDS, 2, jblock), jnp.bfloat16),
        in_specs=[pl.BlockSpec(memory_space=pltpu.VMEM)] * (2 * nchunk),
        out_specs=pl.BlockSpec(memory_space=pl.ANY),
        scratch_shapes=[
            pltpu.VMEM((2 * FEEDS, LANES), jnp.float32),
            pltpu.VMEM((jblock, LANES), jnp.bfloat16),
            pltpu.VMEM((LANES, jblock), jnp.bfloat16),
            pltpu.VMEM((2, jblock // LANES, 2 * IBLOCK, LANES), jnp.bfloat16),
            pltpu.SemaphoreType.DMA((2, jblock // LANES)),
        ],
        compiler_params=pltpu.CompilerParams(vmem_limit_bytes=40 << 20),
        name="correlate",
    )(*own, *other)


def plain(voltages, gains):
    rows = lax.axis_size("row")
    cols = lax.axis_size("col")
    feed_dev = voltages.shape[0]
    chans = gains.shape[1]
    sub = max(1, rows // chans)
    pairs = chans * sub // rows
    iblock = FEEDS // sub
    jblock = FEEDS // cols
    window = prototype(TAPS, NFFT)
    table = dft_table(NFFT, chans, NFFT // 8)
    scale = float(NFFT) ** (-0.5)
    blocks = voltages.reshape(feed_dev, -1, NFFT)
    total = jnp.zeros((feed_dev, SPECTRA, NFFT), jnp.float32)
    for tap in range(TAPS):
        total = total + blocks[:, tap : tap + SPECTRA, :].astype(jnp.float32) * window[tap]
    filtered = total.astype(jnp.bfloat16)
    raw = (
        jnp.dot(
            filtered.reshape(feed_dev * SPECTRA, NFFT), table, preferred_element_type=jnp.float32
        )
        * scale
    )
    raw = raw.reshape(feed_dev, SPECTRA, 2 * chans)
    real_part = raw[:, :, :chans]
    imag_part = raw[:, :, chans:]
    gain_re = gains[:, None, :, 0]
    gain_im = gains[:, None, :, 1]
    out_re = gain_re * real_part - gain_im * imag_part
    out_im = gain_re * imag_part + gain_im * real_part
    stacked = jnp.stack([out_re, out_im], axis=0)
    spectra = (
        jnp.transpose(stacked, (3, 1, 0, 2))
        .reshape(chans, feed_dev, 2 * SPECTRA)
        .astype(jnp.bfloat16)
    )
    outgoing = jnp.repeat(spectra, sub, axis=0)
    turned = lax.all_to_all(outgoing, "row", split_axis=0, concat_axis=1, tiled=True)
    turned = turned.reshape(pairs, rows, feed_dev, 2 * SPECTRA)
    gathered = lax.all_gather(turned, "col", axis=2, tiled=True)
    gathered = gathered.reshape(pairs, FEEDS, 2 * SPECTRA)
    pair_index = lax.axis_index("row") * pairs + jnp.arange(pairs)
    starts = pair_index % sub * iblock

    def first_rows(chan_rows, start):
        return lax.dynamic_slice_in_dim(chan_rows, start, iblock, 0)

    left = jax.vmap(first_rows)(gathered, starts)
    second = lax.dynamic_slice_in_dim(gathered, lax.axis_index("col") * jblock, jblock, 1)
    turned_second = jnp.concatenate([-second[:, :, SPECTRA:], second[:, :, :SPECTRA]], axis=2)
    right = jnp.concatenate([second, turned_second], axis=1)
    product = jnp.einsum("pis,pjs->pij", left, right, preferred_element_type=jnp.float32) / SPECTRA
    return product.astype(jnp.bfloat16).reshape(pairs, iblock, 2, jblock)


def shards(voltages, gains):
    rows = lax.axis_size("row")
    cols = lax.axis_size("col")
    fd = voltages.shape[0]
    chans = gains.shape[1]
    if fd % LANES or chans != LANES // 4 or chans % rows or cols != 2 or rows % cols:
        return plain(voltages, gains)
    pairs = chans // rows
    w = weights(chans)
    gt = gains.transpose(1, 2, 0).reshape(2 * chans, fd)
    own, other = [], []
    first = 0
    for share in CHUNKS:
        fb = fd * share // sum(CHUNKS)
        sp = channelize(voltages, w, gt, first, fb)
        first += fb
        t = lax.all_to_all(sp, "row", split_axis=0, concat_axis=0, tiled=True)
        own.append(t)
        other.append(lax.ppermute(t, "col", [(i, (i + 1) % cols) for i in range(cols)]))
    return correlate(own, other, rows, pairs)


def solution(mesh):
    placed = (P(("band", "row", "col"), None), P(("band", "row", "col"), None, None))
    return jax.shard_map(
        shards,
        mesh=mesh,
        in_specs=placed,
        out_specs=P(("band", "row"), None, None, "col"),
        check_vma=False,
    )
```

```python
import math, functools
import jax
import jax.numpy as jnp
from jax import lax
from jax.experimental import pallas as pl
from jax.experimental.pallas import tpu as pltpu
from jax.sharding import PartitionSpec as P

FEEDS = 2048
NFFT = 2048
TAPS = 16
SPECTRA = 64
QUAD = 4
LANES = 128
UBLOCK = 17


def prototype(taps, length):
    total = taps * length
    index = jnp.arange(total).astype(jnp.float32)
    offset = (index - (total - 1) / 2.0) / length
    window = 0.5 - 0.5 * jnp.cos(2.0 * math.pi * (index + 0.5) / total)
    return (jnp.sinc(offset) * window).reshape(taps, length)


def dft_table(length, chans, first):
    sample = jnp.arange(length)
    channel = first + jnp.arange(chans)
    phase = sample[:, None] * channel[None, :] % length
    angle = phase.astype(jnp.float32) * (2.0 * math.pi / length)
    return jnp.concatenate([jnp.cos(angle), -jnp.sin(angle)], axis=1).astype(jnp.bfloat16)


def fill_weights(h_ref, w, parts, chans, first_chan):
    wide = 2 * chans
    columns = QUAD * wide
    h = h_ref[...]
    hi = h.astype(jnp.bfloat16).astype(jnp.float32)
    mid = (h - hi).astype(jnp.bfloat16).astype(jnp.float32)
    low = h - hi - mid
    rest = jnp.zeros((LANES - 3 * TAPS, NFFT), jnp.float32)
    parts[...] = jnp.concatenate([hi, mid, low, rest], axis=0).T.astype(jnp.bfloat16)
    coarse = NFFT // SPLIT

    def tables(count, step):
        sample = lax.broadcasted_iota(jnp.int32, (count, columns), 0) * step
        channel = first_chan + lax.broadcasted_iota(jnp.int32, (count, columns), 1) % chans
        angle = (sample * channel % NFFT).astype(jnp.float32) * (2.0 * math.pi / NFFT)
        return jnp.cos(angle), jnp.sin(angle)
    fine_cos, fine_sin = tables(SPLIT, 1)
    far_cos, far_sin = tables(coarse, SPLIT)
    real = lax.broadcasted_iota(jnp.int32, (coarse, columns), 1) % wide < chans
    far_one = jnp.where(real, far_cos, -far_sin)
    far_two = jnp.where(real, -far_sin, -far_cos)
    row = lax.broadcasted_iota(jnp.int32, (LANES, columns), 0)
    tap = lax.broadcasted_iota(jnp.int32, (LANES, columns), 1) // wide
    picks = [
        jnp.where((row < 3 * TAPS) & (row % TAPS == QUAD * p + tap), 1.0, 0.0).astype(jnp.bfloat16)
        for p in range(TAPS // QUAD)
    ]
    for block in range(coarse):
        table = far_one[block:block + 1] * fine_cos + far_two[block:block + 1] * fine_sin
        table = table.astype(jnp.bfloat16).astype(jnp.float32)
        rows = slice(block * SPLIT, (block + 1) * SPLIT)
        for p in range(TAPS // QUAD):
            window = jnp.dot(parts[rows, :], picks[p], preferred_element_type=jnp.float32)
            w[p, rows, :] = (window * table).astype(jnp.bfloat16)


def spectra_rows(acc, r0, r1, g1, g2, start, count, fb):
    lane = lax.broadcasted_iota(jnp.int32, (fb, LANES), 1)

    def pair(s):
        at = pl.multiple_of((start + s) * fb, fb)
        two = pl.multiple_of((start + s + 2) * fb, fb)
        return acc[pl.ds(at, fb), 0:LANES] + acc[pl.ds(two, fb), LANES:2 * LANES]
    here = pair(0)
    for s in range(count):
        after = pair(s + 1)
        c = jnp.where(lane < LANES // 2, here, after)
        y = c + pltpu.roll(c, LANES // 2, 1)
        sw = pltpu.roll(y, LANES // 4, 1)
        at = pl.multiple_of((start + s) * fb, fb)
        r0[pl.ds(at, fb), :] = g1 * y + g2 * sw
        r1[pl.ds(at, fb), :] = g1 * sw - g2 * y
        here = after


def channelize_kernel(v_ref, h_ref, g_ref, o_ref, x, w, parts, acc, r0, r1, st, sem, *, first, fb, frames, chans):
    groups = TAPS // QUAD
    region = sum(CHAINS)
    reach = QUAD * (groups - 1)
    count = -(-(SPECTRA + QUAD - 1) // region)

    def copy(j):
        return pltpu.make_async_copy(
            v_ref.at[pl.ds(first, fb), pl.ds(j * NFFT, NFFT)], x.at[pl.ds(j * fb, fb), :], sem.at[j])
    for j in range(frames):
        copy(j).start()
    fill_weights(h_ref, w, parts, chans, NFFT // 8)
    scale = float(NFFT) ** -0.5
    gre = g_ref[pl.ds(0, chans, stride=2), :] * scale
    gim = g_ref[pl.ds(1, chans, stride=2), :] * scale
    g1 = jnp.concatenate([gre] * 4, axis=0).T[first:first + fb]
    g2 = jnp.concatenate([-gim, gim, -gim, gim], axis=0).T[first:first + fb]

    def wait(j, _):
        copy(j).wait()
        return 0
    lax.fori_loop(0, reach, wait, 0)

    def step(i, _):
        lax.fori_loop(i * region + reach, jnp.minimum((i + 1) * region + reach, frames), wait, 0)
        spectra_rows(acc, r0, r1, g1, g2, i * region, region, fb)
        at = 0
        for un in CHAINS:
            total = None
            for p in range(groups):
                start = pl.multiple_of((i * region + at + QUAD * p) * fb, fb)
                d = jnp.dot(x[pl.ds(start, un * fb), :], w[p], preferred_element_type=jnp.float32)
                total = d if total is None else total + d
            acc[pl.ds(pl.multiple_of((PAD + i * region + at) * fb, fb), un * fb), :] = total
            at += un
        return 0
    lax.fori_loop(0, count, step, 0)
    spectra_rows(acc, r0, r1, g1, g2, count * region, SPECTRA + PAD - count * region, fb)
    block = lax.broadcasted_iota(jnp.int32, (SPECTRA, LANES), 1) // chans

    def pick(parts):
        return jnp.where(block < 2, jnp.where(block < 1, parts[0], parts[1]), jnp.where(block < 3, parts[2], parts[3]))

    def turn(f, _):
        def rows(ref, b):
            return ref[pl.ds(PAD * fb + f * 4 + b, SPECTRA, stride=fb), :]
        same = [rows(r0, b) for b in range(4)]
        swap = [rows(r1, b) for b in range(4)]
        top = pick([same[0], swap[1], same[2], swap[3]])
        low = pick([swap[0], same[1], swap[2], same[3]])
        t = jnp.concatenate([top, low], axis=0).T
        for b in range(4):
            st[pl.ds(f * 4 + b, chans, stride=fb), :] = t[b * chans:(b + 1) * chans]
        return 0
    lax.fori_loop(0, fb // 4, turn, 0, unroll=4)
    o_ref[...] = st[...].astype(jnp.bfloat16).reshape(o_ref.shape)


CHAINS = (9, 8)
PAD = sum(CHAINS) + QUAD - 1
SPLIT = 64
CHUNKS = (5, 3)


def channelize(voltages, h, gt, first, fb):
    frames = voltages.shape[1] // NFFT
    chans = gt.shape[0] // 2
    columns = QUAD * 2 * chans
    region = sum(CHAINS)
    slots = -(-(SPECTRA + QUAD - 1) // region) * region
    return pl.pallas_call(
        functools.partial(channelize_kernel, first=first, fb=fb, frames=frames, chans=chans),
        out_shape=jax.ShapeDtypeStruct((chans, fb, 2 * SPECTRA), jnp.bfloat16),
        in_specs=[pl.BlockSpec(memory_space=pl.ANY), pl.BlockSpec(memory_space=pltpu.VMEM), pl.BlockSpec(memory_space=pltpu.VMEM)],
        out_specs=pl.BlockSpec(memory_space=pltpu.VMEM),
        scratch_shapes=[
            pltpu.VMEM(((slots + TAPS - QUAD) * fb, NFFT), jnp.bfloat16),
            pltpu.VMEM((TAPS // QUAD, NFFT, columns), jnp.bfloat16),
            pltpu.VMEM((NFFT, LANES), jnp.bfloat16),
            pltpu.VMEM(((PAD + slots) * fb, columns), jnp.float32),
            pltpu.VMEM(((PAD + SPECTRA) * fb, LANES), jnp.float32),
            pltpu.VMEM(((PAD + SPECTRA) * fb, LANES), jnp.float32),
            pltpu.VMEM((chans * fb, LANES), jnp.float32),
            pltpu.SemaphoreType.DMA((frames,)),
        ],
        compiler_params=pltpu.CompilerParams(vmem_limit_bytes=58 << 20),
        cost_estimate=pl.CostEstimate(flops=2 * slots * fb * TAPS // QUAD * NFFT * columns, bytes_accessed=fb * frames * NFFT * 2, transcendentals=0),
        name="channelize",
    )(voltages, h, gt)


IBLOCK = 512
NSPLIT = 4


def correlate_kernel(*refs, nchunk, rows, pairs):
    own, other = refs[:nchunk], refs[nchunk:2 * nchunk]
    o_ref, lf, right, turned, out, sem = refs[2 * nchunk:]
    col = lax.axis_index("col")
    sizes = [ref.shape[1] for ref in own]
    starts = [sum(sizes[:a]) for a in range(nchunk)]
    fd = sum(sizes)
    nblk = FEEDS // IBLOCK
    jblock = right.shape[0]
    jtiles = jblock // LANES
    half = rows * 2 * fd // jblock

    def put(q, blk, slot, jt):
        return pltpu.make_async_copy(
            out.at[slot, jt], o_ref.reshape(pairs, 2 * FEEDS, jblock).at[q, pl.ds(blk * 2 * IBLOCK, 2 * IBLOCK), pl.ds(jt * LANES, LANES)], sem.at[slot, jt])

    def channel(q, _):
        for r in range(rows):
            for a in range(nchunk):
                for which in range(2):
                    piece = (own if which == 0 else other)[a][r * pairs + q].astype(jnp.float32)
                    c = col if which == 0 else 1 - col
                    fb = sizes[a]
                    lane = lax.broadcasted_iota(jnp.int32, (fb, LANES), 1)
                    sign = jnp.where(lane < SPECTRA, 1.0, -1.0) * (1.0 / SPECTRA)
                    base = pl.multiple_of((r * 2 * fd + c * fd + starts[a]) * 2, LANES // 4)
                    lf[pl.ds(base, fb, stride=2), :] = piece * (1.0 / SPECTRA)
                    lf[pl.ds(base + 1, fb, stride=2), :] = pltpu.roll(piece, SPECTRA, 1) * sign
        for r in range(rows // half):
            for a in range(nchunk):
                for which in range(2):
                    c = col if which == 0 else 1 - col
                    piece = (own if which == 0 else other)[a][(col * (rows // half) + r) * pairs + q]
                    base = pl.multiple_of(r * 2 * fd + c * fd + starts[a], LANES // 8)
                    right[pl.ds(base, sizes[a]), :] = piece
        turned[...] = right[...].T

        def block(blk, _):
            step = q * nblk + blk
            slot = lax.rem(step, 2)

            @pl.when(step >= 2)
            def _():
                for jt in range(jtiles):
                    put(0, 0, slot, jt).wait()
            start = pl.multiple_of(blk * 2 * IBLOCK, 2 * IBLOCK)
            rowsb = lf[pl.ds(start, 2 * IBLOCK), :].astype(jnp.bfloat16)
            width = jblock // NSPLIT
            for k in range(NSPLIT):
                prod = jnp.dot(rowsb, turned[:, k * width:(k + 1) * width], preferred_element_type=jnp.float32).astype(jnp.bfloat16)
                for jt in range(width // LANES):
                    out[slot, k * (width // LANES) + jt] = prod[:, jt * LANES:(jt + 1) * LANES]
                    put(q, blk, slot, k * (width // LANES) + jt).start()
            return 0
        lax.fori_loop(0, nblk, block, 0)
        return 0
    lax.fori_loop(0, pairs, channel, 0)
    for slot in range(2):
        for jt in range(jtiles):
            put(0, 0, slot, jt).wait()


def correlate(own, other, rows, pairs):
    nchunk = len(own)
    jblock = FEEDS // 2
    return pl.pallas_call(
        functools.partial(correlate_kernel, nchunk=nchunk, rows=rows, pairs=pairs),
        out_shape=jax.ShapeDtypeStruct((pairs, FEEDS, 2, jblock), jnp.bfloat16),
        in_specs=[pl.BlockSpec(memory_space=pltpu.VMEM)] * (2 * nchunk),
        out_specs=pl.BlockSpec(memory_space=pl.ANY),
        scratch_shapes=[
            pltpu.VMEM((2 * FEEDS, LANES), jnp.float32),
            pltpu.VMEM((jblock, LANES), jnp.bfloat16),
            pltpu.VMEM((LANES, jblock), jnp.bfloat16),
            pltpu.VMEM((2, jblock // LANES, 2 * IBLOCK, LANES), jnp.bfloat16),
            pltpu.SemaphoreType.DMA((2, jblock // LANES)),
        ],
        compiler_params=pltpu.CompilerParams(vmem_limit_bytes=40 << 20),
        name="correlate",
    )(*own, *other)


def plain(voltages, gains):
    rows = lax.axis_size("row")
    cols = lax.axis_size("col")
    feed_dev = voltages.shape[0]
    chans = gains.shape[1]
    sub = max(1, rows // chans)
    pairs = chans * sub // rows
    iblock = FEEDS // sub
    jblock = FEEDS // cols
    window = prototype(TAPS, NFFT)
    table = dft_table(NFFT, chans, NFFT // 8)
    scale = float(NFFT) ** (-0.5)
    blocks = voltages.reshape(feed_dev, -1, NFFT)
    total = jnp.zeros((feed_dev, SPECTRA, NFFT), jnp.float32)
    for tap in range(TAPS):
        total = total + blocks[:, tap : tap + SPECTRA, :].astype(jnp.float32) * window[tap]
    filtered = total.astype(jnp.bfloat16)
    raw = (
        jnp.dot(
            filtered.reshape(feed_dev * SPECTRA, NFFT), table, preferred_element_type=jnp.float32
        )
        * scale
    )
    raw = raw.reshape(feed_dev, SPECTRA, 2 * chans)
    real_part = raw[:, :, :chans]
    imag_part = raw[:, :, chans:]
    gain_re = gains[:, None, :, 0]
    gain_im = gains[:, None, :, 1]
    out_re = gain_re * real_part - gain_im * imag_part
    out_im = gain_re * imag_part + gain_im * real_part
    stacked = jnp.stack([out_re, out_im], axis=0)
    spectra = (
        jnp.transpose(stacked, (3, 1, 0, 2))
        .reshape(chans, feed_dev, 2 * SPECTRA)
        .astype(jnp.bfloat16)
    )
    outgoing = jnp.repeat(spectra, sub, axis=0)
    turned = lax.all_to_all(outgoing, "row", split_axis=0, concat_axis=1, tiled=True)
    turned = turned.reshape(pairs, rows, feed_dev, 2 * SPECTRA)
    gathered = lax.all_gather(turned, "col", axis=2, tiled=True)
    gathered = gathered.reshape(pairs, FEEDS, 2 * SPECTRA)
    pair_index = lax.axis_index("row") * pairs + jnp.arange(pairs)
    starts = pair_index % sub * iblock

    def first_rows(chan_rows, start):
        return lax.dynamic_slice_in_dim(chan_rows, start, iblock, 0)

    left = jax.vmap(first_rows)(gathered, starts)
    second = lax.dynamic_slice_in_dim(gathered, lax.axis_index("col") * jblock, jblock, 1)
    turned_second = jnp.concatenate([-second[:, :, SPECTRA:], second[:, :, :SPECTRA]], axis=2)
    right = jnp.concatenate([second, turned_second], axis=1)
    product = jnp.einsum("pis,pjs->pij", left, right, preferred_element_type=jnp.float32) / SPECTRA
    return product.astype(jnp.bfloat16).reshape(pairs, iblock, 2, jblock)


def shards(voltages, gains):
    rows = lax.axis_size("row")
    cols = lax.axis_size("col")
    fd = voltages.shape[0]
    chans = gains.shape[1]
    if fd % LANES or chans != LANES // 4 or chans % rows or cols != 2 or rows % cols:
        return plain(voltages, gains)
    pairs = chans // rows
    h = prototype(TAPS, NFFT)
    gt = gains.transpose(1, 2, 0).reshape(2 * chans, fd)
    own, other = [], []
    first = 0
    for share in CHUNKS:
        fb = fd * share // sum(CHUNKS)
        sp = channelize(voltages, h, gt, first, fb)
        first += fb
        t = lax.all_to_all(sp, "row", split_axis=0, concat_axis=0, tiled=True)
        own.append(t)
        other.append(lax.ppermute(t, "col", [(i, (i + 1) % cols) for i in range(cols)]))
    return correlate(own, other, rows, pairs)


def solution(mesh):
    placed = (P(("band", "row", "col"), None), P(("band", "row", "col"), None, None))
    return jax.shard_map(
        shards,
        mesh=mesh,
        in_specs=placed,
        out_specs=P(("band", "row"), None, None, "col"),
        check_vma=False,
    )
```

```python
import math, functools
import jax
import jax.numpy as jnp
from jax import lax
from jax.experimental import pallas as pl
from jax.experimental.pallas import tpu as pltpu
from jax.sharding import PartitionSpec as P

FEEDS = 2048
NFFT = 2048
TAPS = 16
SPECTRA = 64
QUAD = 4
LANES = 128
UBLOCK = 17


def prototype(taps, length):
    total = taps * length
    index = jnp.arange(total).astype(jnp.float32)
    offset = (index - (total - 1) / 2.0) / length
    window = 0.5 - 0.5 * jnp.cos(2.0 * math.pi * (index + 0.5) / total)
    return (jnp.sinc(offset) * window).reshape(taps, length)


def dft_table(length, chans, first):
    sample = jnp.arange(length)
    channel = first + jnp.arange(chans)
    phase = sample[:, None] * channel[None, :] % length
    angle = phase.astype(jnp.float32) * (2.0 * math.pi / length)
    return jnp.concatenate([jnp.cos(angle), -jnp.sin(angle)], axis=1).astype(jnp.bfloat16)


def fill_weights(w, parts, chans, first_chan):
    wide = 2 * chans
    columns = QUAD * wide
    length = TAPS * NFFT
    index = lax.broadcasted_iota(jnp.int32, (TAPS, NFFT), 0) * NFFT + lax.broadcasted_iota(jnp.int32, (TAPS, NFFT), 1)
    index = index.astype(jnp.float32)
    offset = math.pi * ((index - (length - 1) / 2.0) / NFFT)
    h = jnp.sin(offset) / offset * (0.5 - 0.5 * jnp.cos(2.0 * math.pi * (index + 0.5) / length))
    hi = h.astype(jnp.bfloat16).astype(jnp.float32)
    mid = (h - hi).astype(jnp.bfloat16).astype(jnp.float32)
    low = h - hi - mid
    rest = jnp.zeros((LANES - 3 * TAPS, NFFT), jnp.float32)
    parts[...] = jnp.concatenate([hi, mid, low, rest], axis=0).T.astype(jnp.bfloat16)
    coarse = NFFT // SPLIT

    def tables(count, step):
        sample = lax.broadcasted_iota(jnp.int32, (count, columns), 0) * step
        channel = first_chan + lax.broadcasted_iota(jnp.int32, (count, columns), 1) % chans
        angle = (sample * channel % NFFT).astype(jnp.float32) * (2.0 * math.pi / NFFT)
        return jnp.cos(angle), jnp.sin(angle)
    fine_cos, fine_sin = tables(SPLIT, 1)
    far_cos, far_sin = tables(coarse, SPLIT)
    real = lax.broadcasted_iota(jnp.int32, (coarse, columns), 1) % wide < chans
    far_one = jnp.where(real, far_cos, -far_sin)
    far_two = jnp.where(real, -far_sin, -far_cos)
    row = lax.broadcasted_iota(jnp.int32, (LANES, columns), 0)
    tap = lax.broadcasted_iota(jnp.int32, (LANES, columns), 1) // wide
    picks = [
        jnp.where((row < 3 * TAPS) & (row % TAPS == QUAD * p + tap), 1.0, 0.0).astype(jnp.bfloat16)
        for p in range(TAPS // QUAD)
    ]
    for block in range(coarse):
        table = far_one[block:block + 1] * fine_cos + far_two[block:block + 1] * fine_sin
        table = table.astype(jnp.bfloat16).astype(jnp.float32)
        rows = slice(block * SPLIT, (block + 1) * SPLIT)
        for p in range(TAPS // QUAD):
            window = jnp.dot(parts[rows, :], picks[p], preferred_element_type=jnp.float32)
            w[p, rows, :] = (window * table).astype(jnp.bfloat16)


def spectra_rows(acc, r0, r1, g1, g2, start, count, fb):
    lane = lax.broadcasted_iota(jnp.int32, (fb, LANES), 1)

    def pair(s):
        at = pl.multiple_of((start + s) * fb, fb)
        two = pl.multiple_of((start + s + 2) * fb, fb)
        return acc[pl.ds(at, fb), 0:LANES] + acc[pl.ds(two, fb), LANES:2 * LANES]
    here = pair(0)
    for s in range(count):
        after = pair(s + 1)
        c = jnp.where(lane < LANES // 2, here, after)
        y = c + pltpu.roll(c, LANES // 2, 1)
        sw = pltpu.roll(y, LANES // 4, 1)
        at = pl.multiple_of((start + s) * fb, fb)
        r0[pl.ds(at, fb), :] = g1 * y + g2 * sw
        r1[pl.ds(at, fb), :] = g1 * sw - g2 * y
        here = after


def channelize_kernel(v_ref, g_ref, *refs, first, fb, frames, chans, rows):
    o_refs = refs[:-8]
    x, w, parts, acc, r0, r1, st, sem = refs[-8:]
    groups = TAPS // QUAD
    region = sum(CHAINS)
    reach = QUAD * (groups - 1)
    count = -(-(SPECTRA + QUAD - 1) // region)

    def copy(j):
        return pltpu.make_async_copy(
            v_ref.at[pl.ds(first, fb), pl.ds(j * NFFT, NFFT)], x.at[pl.ds(j * fb, fb), :], sem.at[j])
    for j in range(frames):
        copy(j).start()
    fill_weights(w, parts, chans, NFFT // 8)
    scale = float(NFFT) ** -0.5
    gre = g_ref[pl.ds(0, chans, stride=2), :] * scale
    gim = g_ref[pl.ds(1, chans, stride=2), :] * scale
    g1 = jnp.concatenate([gre] * 4, axis=0).T[first:first + fb]
    g2 = jnp.concatenate([-gim, gim, -gim, gim], axis=0).T[first:first + fb]

    def wait(j, _):
        copy(j).wait()
        return 0
    lax.fori_loop(0, reach, wait, 0)

    def step(i, _):
        lax.fori_loop(i * region + reach, jnp.minimum((i + 1) * region + reach, frames), wait, 0)
        spectra_rows(acc, r0, r1, g1, g2, i * region, region, fb)
        at = 0
        for un in CHAINS:
            total = None
            for p in range(groups):
                start = pl.multiple_of((i * region + at + QUAD * p) * fb, fb)
                d = jnp.dot(x[pl.ds(start, un * fb), :], w[p], preferred_element_type=jnp.float32)
                total = d if total is None else total + d
            acc[pl.ds(pl.multiple_of((PAD + i * region + at) * fb, fb), un * fb), :] = total
            at += un
        return 0
    lax.fori_loop(0, count, step, 0)
    spectra_rows(acc, r0, r1, g1, g2, count * region, SPECTRA + PAD - count * region, fb)
    block = lax.broadcasted_iota(jnp.int32, (SPECTRA, LANES), 1) // chans

    def pick(parts):
        return jnp.where(block < 2, jnp.where(block < 1, parts[0], parts[1]), jnp.where(block < 3, parts[2], parts[3]))

    def turn(f, _):
        def rows(ref, b):
            return ref[pl.ds(PAD * fb + f * 4 + b, SPECTRA, stride=fb), :]
        same = [rows(r0, b) for b in range(4)]
        swap = [rows(r1, b) for b in range(4)]
        top = pick([same[0], swap[1], same[2], swap[3]])
        low = pick([swap[0], same[1], swap[2], same[3]])
        t = jnp.concatenate([top, low], axis=0).T
        for b in range(4):
            st[pl.ds(f * 4 + b, chans, stride=fb), :] = t[b * chans:(b + 1) * chans]
        return 0
    lax.fori_loop(0, fb // 4, turn, 0, unroll=4)
    if len(o_refs) == 1:
        o_refs[0][...] = st[...].astype(jnp.bfloat16).reshape(o_refs[0].shape)
        return
    share = chans // rows * fb
    for d in range(rows):
        at = pl.multiple_of(lax.rem(lax.axis_index("row") + d, rows) * share, share)
        o_refs[d][...] = st[pl.ds(at, share), :].astype(jnp.bfloat16).reshape(o_refs[d].shape)


CHAINS = (9, 8)
PAD = sum(CHAINS) + QUAD - 1
SPLIT = 64
CHUNKS = (5, 3)


def channelize(voltages, gt, first, fb, rows, pieces):
    frames = voltages.shape[1] // NFFT
    chans = gt.shape[0] // 2
    columns = QUAD * 2 * chans
    region = sum(CHAINS)
    slots = -(-(SPECTRA + QUAD - 1) // region) * region
    return pl.pallas_call(
        functools.partial(channelize_kernel, first=first, fb=fb, frames=frames, chans=chans, rows=rows),
        out_shape=[jax.ShapeDtypeStruct((chans // pieces, fb, 2 * SPECTRA), jnp.bfloat16)] * pieces,
        in_specs=[pl.BlockSpec(memory_space=pl.ANY), pl.BlockSpec(memory_space=pltpu.VMEM)],
        out_specs=[pl.BlockSpec(memory_space=pltpu.VMEM)] * pieces,
        scratch_shapes=[
            pltpu.VMEM(((slots + TAPS - QUAD) * fb, NFFT), jnp.bfloat16),
            pltpu.VMEM((TAPS // QUAD, NFFT, columns), jnp.bfloat16),
            pltpu.VMEM((NFFT, LANES), jnp.bfloat16),
            pltpu.VMEM(((PAD + slots) * fb, columns), jnp.float32),
            pltpu.VMEM(((PAD + SPECTRA) * fb, LANES), jnp.float32),
            pltpu.VMEM(((PAD + SPECTRA) * fb, LANES), jnp.float32),
            pltpu.VMEM((chans * fb, LANES), jnp.float32),
            pltpu.SemaphoreType.DMA((frames,)),
        ],
        compiler_params=pltpu.CompilerParams(vmem_limit_bytes=58 << 20),
        cost_estimate=pl.CostEstimate(flops=2 * slots * fb * TAPS // QUAD * NFFT * columns, bytes_accessed=fb * frames * NFFT * 2, transcendentals=0),
        name="channelize",
    )(voltages, gt)


IBLOCK = 1024
NSPLIT = 4


def correlate_kernel(*refs, nchunk, rows, pairs, orders):
    own, other = refs[:nchunk], refs[nchunk:2 * nchunk]
    o_ref, lf, right, turned, out, sem = refs[2 * nchunk:]
    col = lax.axis_index("col")
    me = lax.axis_index("row")

    def place(a, r):
        return (lax.rem(me - r + rows, rows) if orders[a] else r) * pairs
    sizes = [ref.shape[1] for ref in own]
    starts = [sum(sizes[:a]) for a in range(nchunk)]
    fd = sum(sizes)
    nblk = FEEDS // IBLOCK
    jblock = right.shape[0]
    jtiles = jblock // LANES
    half = rows * 2 * fd // jblock

    def put(q, blk, slot, jt):
        return pltpu.make_async_copy(
            out.at[slot, jt], o_ref.reshape(pairs, 2 * FEEDS, jblock).at[q, pl.ds(blk * 2 * IBLOCK, 2 * IBLOCK), pl.ds(jt * LANES, LANES)], sem.at[slot, jt])

    def channel(q, _):
        for r in range(rows):
            for a in range(nchunk):
                for which in range(2):
                    piece = (own if which == 0 else other)[a][place(a, r) + q].astype(jnp.float32)
                    c = col if which == 0 else 1 - col
                    fb = sizes[a]
                    lane = lax.broadcasted_iota(jnp.int32, (fb, LANES), 1)
                    sign = jnp.where(lane < SPECTRA, 1.0, -1.0) * (1.0 / SPECTRA)
                    base = pl.multiple_of((r * 2 * fd + c * fd + starts[a]) * 2, LANES // 4)
                    lf[pl.ds(base, fb, stride=2), :] = piece * (1.0 / SPECTRA)
                    lf[pl.ds(base + 1, fb, stride=2), :] = pltpu.roll(piece, SPECTRA, 1) * sign
        for r in range(rows // half):
            for a in range(nchunk):
                for which in range(2):
                    c = col if which == 0 else 1 - col
                    piece = (own if which == 0 else other)[a][place(a, col * (rows // half) + r) + q]
                    base = pl.multiple_of(r * 2 * fd + c * fd + starts[a], LANES // 8)
                    right[pl.ds(base, sizes[a]), :] = piece
        turned[...] = right[...].T

        def block(blk, _):
            step = q * nblk + blk
            slot = lax.rem(step, 2)

            @pl.when(step >= 2)
            def _():
                for jt in range(jtiles):
                    put(0, 0, slot, jt).wait()
            start = pl.multiple_of(blk * 2 * IBLOCK, 2 * IBLOCK)
            rowsb = lf[pl.ds(start, 2 * IBLOCK), :].astype(jnp.bfloat16)
            width = jblock // NSPLIT
            for k in range(NSPLIT):
                prod = jnp.dot(rowsb, turned[:, k * width:(k + 1) * width], preferred_element_type=jnp.float32).astype(jnp.bfloat16)
                for jt in range(width // LANES):
                    out[slot, k * (width // LANES) + jt] = prod[:, jt * LANES:(jt + 1) * LANES]
                    put(q, blk, slot, k * (width // LANES) + jt).start()
            return 0
        lax.fori_loop(0, nblk, block, 0)
        return 0
    lax.fori_loop(0, pairs, channel, 0)
    for slot in range(2):
        for jt in range(jtiles):
            put(0, 0, slot, jt).wait()


def correlate(own, other, rows, pairs, orders):
    nchunk = len(own)
    jblock = FEEDS // 2
    return pl.pallas_call(
        functools.partial(correlate_kernel, nchunk=nchunk, rows=rows, pairs=pairs, orders=orders),
        out_shape=jax.ShapeDtypeStruct((pairs, FEEDS, 2, jblock), jnp.bfloat16),
        in_specs=[pl.BlockSpec(memory_space=pltpu.VMEM)] * (2 * nchunk),
        out_specs=pl.BlockSpec(memory_space=pl.ANY),
        scratch_shapes=[
            pltpu.VMEM((2 * FEEDS, LANES), jnp.float32),
            pltpu.VMEM((jblock, LANES), jnp.bfloat16),
            pltpu.VMEM((LANES, jblock), jnp.bfloat16),
            pltpu.VMEM((2, jblock // LANES, 2 * IBLOCK, LANES), jnp.bfloat16),
            pltpu.SemaphoreType.DMA((2, jblock // LANES)),
        ],
        compiler_params=pltpu.CompilerParams(vmem_limit_bytes=40 << 20),
        name="correlate",
    )(*own, *other)


def plain(voltages, gains):
    rows = lax.axis_size("row")
    cols = lax.axis_size("col")
    feed_dev = voltages.shape[0]
    chans = gains.shape[1]
    sub = max(1, rows // chans)
    pairs = chans * sub // rows
    iblock = FEEDS // sub
    jblock = FEEDS // cols
    window = prototype(TAPS, NFFT)
    table = dft_table(NFFT, chans, NFFT // 8)
    scale = float(NFFT) ** (-0.5)
    blocks = voltages.reshape(feed_dev, -1, NFFT)
    total = jnp.zeros((feed_dev, SPECTRA, NFFT), jnp.float32)
    for tap in range(TAPS):
        total = total + blocks[:, tap : tap + SPECTRA, :].astype(jnp.float32) * window[tap]
    filtered = total.astype(jnp.bfloat16)
    raw = (
        jnp.dot(
            filtered.reshape(feed_dev * SPECTRA, NFFT), table, preferred_element_type=jnp.float32
        )
        * scale
    )
    raw = raw.reshape(feed_dev, SPECTRA, 2 * chans)
    real_part = raw[:, :, :chans]
    imag_part = raw[:, :, chans:]
    gain_re = gains[:, None, :, 0]
    gain_im = gains[:, None, :, 1]
    out_re = gain_re * real_part - gain_im * imag_part
    out_im = gain_re * imag_part + gain_im * real_part
    stacked = jnp.stack([out_re, out_im], axis=0)
    spectra = (
        jnp.transpose(stacked, (3, 1, 0, 2))
        .reshape(chans, feed_dev, 2 * SPECTRA)
        .astype(jnp.bfloat16)
    )
    outgoing = jnp.repeat(spectra, sub, axis=0)
    turned = lax.all_to_all(outgoing, "row", split_axis=0, concat_axis=1, tiled=True)
    turned = turned.reshape(pairs, rows, feed_dev, 2 * SPECTRA)
    gathered = lax.all_gather(turned, "col", axis=2, tiled=True)
    gathered = gathered.reshape(pairs, FEEDS, 2 * SPECTRA)
    pair_index = lax.axis_index("row") * pairs + jnp.arange(pairs)
    starts = pair_index % sub * iblock

    def first_rows(chan_rows, start):
        return lax.dynamic_slice_in_dim(chan_rows, start, iblock, 0)

    left = jax.vmap(first_rows)(gathered, starts)
    second = lax.dynamic_slice_in_dim(gathered, lax.axis_index("col") * jblock, jblock, 1)
    turned_second = jnp.concatenate([-second[:, :, SPECTRA:], second[:, :, :SPECTRA]], axis=2)
    right = jnp.concatenate([second, turned_second], axis=1)
    product = jnp.einsum("pis,pjs->pij", left, right, preferred_element_type=jnp.float32) / SPECTRA
    return product.astype(jnp.bfloat16).reshape(pairs, iblock, 2, jblock)


def shards(voltages, gains):
    rows = lax.axis_size("row")
    cols = lax.axis_size("col")
    fd = voltages.shape[0]
    chans = gains.shape[1]
    if fd % LANES or chans != LANES // 4 or chans % rows or cols != 2 or rows % cols:
        return plain(voltages, gains)
    pairs = chans // rows
    gt = gains.transpose(1, 2, 0).reshape(2 * chans, fd)
    own, other, orders = [], [], []
    first = 0
    for number, share in enumerate(CHUNKS):
        fb = fd * share // sum(CHUNKS)
        final = number + 1 == len(CHUNKS)
        sent = channelize(voltages, gt, first, fb, rows, rows if final else 1)
        sent, gt = lax.optimization_barrier((list(sent), gt))
        first += fb
        if final:
            got = [sent[0]]
            for d in range(1, rows):
                got.append(lax.ppermute(sent[d], "row", [(i, (i + d) % rows) for i in range(rows)]))
            t = jnp.concatenate(got, axis=0)
        else:
            t = lax.all_to_all(sent[0], "row", split_axis=0, concat_axis=0, tiled=True)
        own.append(t)
        other.append(lax.ppermute(t, "col", [(i, (i + 1) % cols) for i in range(cols)]))
        orders.append(final)
    return correlate(own, other, rows, pairs, tuple(orders))


def solution(mesh):
    placed = (P(("band", "row", "col"), None), P(("band", "row", "col"), None, None))
    return jax.shard_map(
        shards,
        mesh=mesh,
        in_specs=placed,
        out_specs=P(("band", "row"), None, None, "col"),
        check_vma=False,
    )
```

```python
import math, functools
import jax
import jax.numpy as jnp
from jax import lax
from jax.experimental import pallas as pl
from jax.experimental.pallas import tpu as pltpu
from jax.sharding import PartitionSpec as P

FEEDS = 2048
NFFT = 2048
TAPS = 16
SPECTRA = 64
QUAD = 4
LANES = 128
UBLOCK = 17


def prototype(taps, length):
    total = taps * length
    index = jnp.arange(total).astype(jnp.float32)
    offset = (index - (total - 1) / 2.0) / length
    window = 0.5 - 0.5 * jnp.cos(2.0 * math.pi * (index + 0.5) / total)
    return (jnp.sinc(offset) * window).reshape(taps, length)


def dft_table(length, chans, first):
    sample = jnp.arange(length)
    channel = first + jnp.arange(chans)
    phase = sample[:, None] * channel[None, :] % length
    angle = phase.astype(jnp.float32) * (2.0 * math.pi / length)
    return jnp.concatenate([jnp.cos(angle), -jnp.sin(angle)], axis=1).astype(jnp.bfloat16)


def fill_weights(w, parts, chans, first_chan):
    wide = 2 * chans
    columns = QUAD * wide
    length = TAPS * NFFT
    index = lax.broadcasted_iota(jnp.int32, (TAPS, NFFT), 0) * NFFT + lax.broadcasted_iota(jnp.int32, (TAPS, NFFT), 1)
    index = index.astype(jnp.float32)
    offset = math.pi * ((index - (length - 1) / 2.0) / NFFT)
    h = jnp.sin(offset) / offset * (0.5 - 0.5 * jnp.cos(2.0 * math.pi * (index + 0.5) / length))
    hi = h.astype(jnp.bfloat16).astype(jnp.float32)
    mid = (h - hi).astype(jnp.bfloat16).astype(jnp.float32)
    low = h - hi - mid
    rest = jnp.zeros((LANES - 3 * TAPS, NFFT), jnp.float32)
    parts[...] = jnp.concatenate([hi, mid, low, rest], axis=0).T.astype(jnp.bfloat16)
    coarse = NFFT // SPLIT

    def tables(count, step):
        sample = lax.broadcasted_iota(jnp.int32, (count, columns), 0) * step
        channel = first_chan + lax.broadcasted_iota(jnp.int32, (count, columns), 1) % chans
        angle = (sample * channel % NFFT).astype(jnp.float32) * (2.0 * math.pi / NFFT)
        return jnp.cos(angle), jnp.sin(angle)
    fine_cos, fine_sin = tables(SPLIT, 1)
    far_cos, far_sin = tables(coarse, SPLIT)
    real = lax.broadcasted_iota(jnp.int32, (coarse, columns), 1) % wide < chans
    far_one = jnp.where(real, far_cos, -far_sin)
    far_two = jnp.where(real, -far_sin, -far_cos)
    row = lax.broadcasted_iota(jnp.int32, (LANES, columns), 0)
    tap = lax.broadcasted_iota(jnp.int32, (LANES, columns), 1) // wide
    picks = [
        jnp.where((row < 3 * TAPS) & (row % TAPS == QUAD * p + tap), 1.0, 0.0).astype(jnp.bfloat16)
        for p in range(TAPS // QUAD)
    ]
    for block in range(coarse):
        table = far_one[block:block + 1] * fine_cos + far_two[block:block + 1] * fine_sin
        table = table.astype(jnp.bfloat16).astype(jnp.float32)
        rows = slice(block * SPLIT, (block + 1) * SPLIT)
        for p in range(TAPS // QUAD):
            window = jnp.dot(parts[rows, :], picks[p], preferred_element_type=jnp.float32)
            w[p, rows, :] = (window * table).astype(jnp.bfloat16)


def spectra_rows(acc, r0, r1, g1, g2, start, count, fb):
    lane = lax.broadcasted_iota(jnp.int32, (fb, LANES), 1)

    def pair(s):
        at = pl.multiple_of((start + s) * fb, fb)
        two = pl.multiple_of((start + s + 2) * fb, fb)
        return acc[pl.ds(at, fb), 0:LANES] + acc[pl.ds(two, fb), LANES:2 * LANES]
    here = pair(0)
    for s in range(count):
        after = pair(s + 1)
        c = jnp.where(lane < LANES // 2, here, after)
        y = c + pltpu.roll(c, LANES // 2, 1)
        sw = pltpu.roll(y, LANES // 4, 1)
        at = pl.multiple_of((start + s) * fb, fb)
        r0[pl.ds(at, fb), :] = g1 * y + g2 * sw
        r1[pl.ds(at, fb), :] = g1 * sw - g2 * y
        here = after


def channelize_kernel(v_ref, g_ref, *refs, first, fb, frames, chans, rows):
    o_refs = refs[:-8]
    x, w, parts, acc, r0, r1, st, sem = refs[-8:]
    groups = TAPS // QUAD
    region = REGION
    half = region * fb // 32 * 16
    reach = QUAD * (groups - 1)
    count = -(-(SPECTRA + QUAD - 1) // region)

    def copy(j):
        return pltpu.make_async_copy(
            v_ref.at[pl.ds(first, fb), pl.ds(j * NFFT, NFFT)], x.at[pl.ds(j * fb, fb), :], sem.at[j])
    for j in range(frames):
        copy(j).start()
    fill_weights(w, parts, chans, NFFT // 8)
    scale = float(NFFT) ** -0.5
    gre = g_ref[pl.ds(0, chans, stride=2), :] * scale
    gim = g_ref[pl.ds(1, chans, stride=2), :] * scale
    g1 = jnp.concatenate([gre] * 4, axis=0).T[first:first + fb]
    g2 = jnp.concatenate([-gim, gim, -gim, gim], axis=0).T[first:first + fb]

    def wait(j, _):
        copy(j).wait()
        return 0
    lax.fori_loop(0, reach, wait, 0)

    def step(i, _):
        lax.fori_loop(i * region + reach, jnp.minimum((i + 1) * region + reach, frames), wait, 0)
        spectra_rows(acc, r0, r1, g1, g2, i * region, region, fb)
        for at, size in ((0, half), (half, region * fb - half)):
            total = None
            for p in range(groups):
                start = pl.multiple_of((i * region + QUAD * p) * fb + at, 16)
                d = jnp.dot(x[pl.ds(start, size), :], w[p], preferred_element_type=jnp.float32)
                total = d if total is None else total + d
            acc[pl.ds(pl.multiple_of((PAD + i * region) * fb + at, 16), size), :] = total
        return 0
    lax.fori_loop(0, count, step, 0)
    spectra_rows(acc, r0, r1, g1, g2, count * region, SPECTRA + PAD - count * region, fb)
    block = lax.broadcasted_iota(jnp.int32, (SPECTRA, LANES), 1) // chans

    def pick(parts):
        return jnp.where(block < 2, jnp.where(block < 1, parts[0], parts[1]), jnp.where(block < 3, parts[2], parts[3]))

    def turn(f, _):
        def rows(ref, b):
            return ref[pl.ds(PAD * fb + f * 4 + b, SPECTRA, stride=fb), :]
        same = [rows(r0, b) for b in range(4)]
        swap = [rows(r1, b) for b in range(4)]
        top = pick([same[0], swap[1], same[2], swap[3]])
        low = pick([swap[0], same[1], swap[2], same[3]])
        t = jnp.concatenate([top, low], axis=0).T
        for b in range(4):
            st[pl.ds(f * 4 + b, chans, stride=fb), :] = t[b * chans:(b + 1) * chans]
        return 0
    lax.fori_loop(0, fb // 4, turn, 0, unroll=4)
    if len(o_refs) == 1:
        o_refs[0][...] = st[...].astype(jnp.bfloat16).reshape(o_refs[0].shape)
        return
    share = chans // rows * fb
    for d in range(rows):
        at = pl.multiple_of(lax.rem(lax.axis_index("row") + d, rows) * share, share)
        o_refs[d][...] = st[pl.ds(at, share), :].astype(jnp.bfloat16).reshape(o_refs[d].shape)


REGION = 17
PAD = REGION + QUAD - 1
SPLIT = 64
CHUNKS = (5, 3)


def channelize(voltages, gt, first, fb, rows, pieces):
    frames = voltages.shape[1] // NFFT
    chans = gt.shape[0] // 2
    columns = QUAD * 2 * chans
    region = REGION
    slots = -(-(SPECTRA + QUAD - 1) // region) * region
    return pl.pallas_call(
        functools.partial(channelize_kernel, first=first, fb=fb, frames=frames, chans=chans, rows=rows),
        out_shape=[jax.ShapeDtypeStruct((chans // pieces, fb, 2 * SPECTRA), jnp.bfloat16)] * pieces,
        in_specs=[pl.BlockSpec(memory_space=pl.ANY), pl.BlockSpec(memory_space=pltpu.VMEM)],
        out_specs=[pl.BlockSpec(memory_space=pltpu.VMEM)] * pieces,
        scratch_shapes=[
            pltpu.VMEM(((slots + TAPS - QUAD) * fb, NFFT), jnp.bfloat16),
            pltpu.VMEM((TAPS // QUAD, NFFT, columns), jnp.bfloat16),
            pltpu.VMEM((NFFT, LANES), jnp.bfloat16),
            pltpu.VMEM(((PAD + slots) * fb, columns), jnp.float32),
            pltpu.VMEM(((PAD + SPECTRA) * fb, LANES), jnp.float32),
            pltpu.VMEM(((PAD + SPECTRA) * fb, LANES), jnp.float32),
            pltpu.VMEM((chans * fb, LANES), jnp.float32),
            pltpu.SemaphoreType.DMA((frames,)),
        ],
        compiler_params=pltpu.CompilerParams(vmem_limit_bytes=58 << 20),
        cost_estimate=pl.CostEstimate(flops=2 * slots * fb * TAPS // QUAD * NFFT * columns, bytes_accessed=fb * frames * NFFT * 2, transcendentals=0),
        name="channelize",
    )(voltages, gt)


IBLOCK = 1024
NSPLIT = 4


def correlate_kernel(*refs, nchunk, rows, pairs, orders):
    own, other = refs[:nchunk], refs[nchunk:2 * nchunk]
    o_ref, lf, right, turned, out, sem = refs[2 * nchunk:]
    col = lax.axis_index("col")
    me = lax.axis_index("row")

    def place(a, r):
        return (lax.rem(me - r + rows, rows) if orders[a] else r) * pairs
    sizes = [ref.shape[1] for ref in own]
    starts = [sum(sizes[:a]) for a in range(nchunk)]
    fd = sum(sizes)
    nblk = FEEDS // IBLOCK
    jblock = right.shape[0]
    jtiles = jblock // LANES
    half = rows * 2 * fd // jblock

    def put(q, blk, slot, jt):
        return pltpu.make_async_copy(
            out.at[slot, jt], o_ref.reshape(pairs, 2 * FEEDS, jblock).at[q, pl.ds(blk * 2 * IBLOCK, 2 * IBLOCK), pl.ds(jt * LANES, LANES)], sem.at[slot, jt])

    def channel(q, _):
        for r in range(rows):
            for a in range(nchunk):
                for which in range(2):
                    piece = (own if which == 0 else other)[a][place(a, r) + q].astype(jnp.float32)
                    c = col if which == 0 else 1 - col
                    fb = sizes[a]
                    lane = lax.broadcasted_iota(jnp.int32, (fb, LANES), 1)
                    sign = jnp.where(lane < SPECTRA, 1.0, -1.0) * (1.0 / SPECTRA)
                    base = pl.multiple_of((r * 2 * fd + c * fd + starts[a]) * 2, LANES // 4)
                    lf[pl.ds(base, fb, stride=2), :] = piece * (1.0 / SPECTRA)
                    lf[pl.ds(base + 1, fb, stride=2), :] = pltpu.roll(piece, SPECTRA, 1) * sign
        for r in range(rows // half):
            for a in range(nchunk):
                for which in range(2):
                    c = col if which == 0 else 1 - col
                    piece = (own if which == 0 else other)[a][place(a, col * (rows // half) + r) + q]
                    base = pl.multiple_of(r * 2 * fd + c * fd + starts[a], LANES // 8)
                    right[pl.ds(base, sizes[a]), :] = piece
        turned[...] = right[...].T

        def block(blk, _):
            step = q * nblk + blk
            slot = lax.rem(step, 2)

            @pl.when(step >= 2)
            def _():
                for jt in range(jtiles):
                    put(0, 0, slot, jt).wait()
            start = pl.multiple_of(blk * 2 * IBLOCK, 2 * IBLOCK)
            rowsb = lf[pl.ds(start, 2 * IBLOCK), :].astype(jnp.bfloat16)
            width = jblock // NSPLIT
            for k in range(NSPLIT):
                prod = jnp.dot(rowsb, turned[:, k * width:(k + 1) * width], preferred_element_type=jnp.float32).astype(jnp.bfloat16)
                for jt in range(width // LANES):
                    out[slot, k * (width // LANES) + jt] = prod[:, jt * LANES:(jt + 1) * LANES]
                    put(q, blk, slot, k * (width // LANES) + jt).start()
            return 0
        lax.fori_loop(0, nblk, block, 0)
        return 0
    lax.fori_loop(0, pairs, channel, 0)
    for slot in range(2):
        for jt in range(jtiles):
            put(0, 0, slot, jt).wait()


def correlate(own, other, rows, pairs, orders):
    nchunk = len(own)
    jblock = FEEDS // 2
    return pl.pallas_call(
        functools.partial(correlate_kernel, nchunk=nchunk, rows=rows, pairs=pairs, orders=orders),
        out_shape=jax.ShapeDtypeStruct((pairs, FEEDS, 2, jblock), jnp.bfloat16),
        in_specs=[pl.BlockSpec(memory_space=pltpu.VMEM)] * (2 * nchunk),
        out_specs=pl.BlockSpec(memory_space=pl.ANY),
        scratch_shapes=[
            pltpu.VMEM((2 * FEEDS, LANES), jnp.float32),
            pltpu.VMEM((jblock, LANES), jnp.bfloat16),
            pltpu.VMEM((LANES, jblock), jnp.bfloat16),
            pltpu.VMEM((2, jblock // LANES, 2 * IBLOCK, LANES), jnp.bfloat16),
            pltpu.SemaphoreType.DMA((2, jblock // LANES)),
        ],
        compiler_params=pltpu.CompilerParams(vmem_limit_bytes=40 << 20),
        name="correlate",
    )(*own, *other)


def plain(voltages, gains):
    rows = lax.axis_size("row")
    cols = lax.axis_size("col")
    feed_dev = voltages.shape[0]
    chans = gains.shape[1]
    sub = max(1, rows // chans)
    pairs = chans * sub // rows
    iblock = FEEDS // sub
    jblock = FEEDS // cols
    window = prototype(TAPS, NFFT)
    table = dft_table(NFFT, chans, NFFT // 8)
    scale = float(NFFT) ** (-0.5)
    blocks = voltages.reshape(feed_dev, -1, NFFT)
    total = jnp.zeros((feed_dev, SPECTRA, NFFT), jnp.float32)
    for tap in range(TAPS):
        total = total + blocks[:, tap : tap + SPECTRA, :].astype(jnp.float32) * window[tap]
    filtered = total.astype(jnp.bfloat16)
    raw = (
        jnp.dot(
            filtered.reshape(feed_dev * SPECTRA, NFFT), table, preferred_element_type=jnp.float32
        )
        * scale
    )
    raw = raw.reshape(feed_dev, SPECTRA, 2 * chans)
    real_part = raw[:, :, :chans]
    imag_part = raw[:, :, chans:]
    gain_re = gains[:, None, :, 0]
    gain_im = gains[:, None, :, 1]
    out_re = gain_re * real_part - gain_im * imag_part
    out_im = gain_re * imag_part + gain_im * real_part
    stacked = jnp.stack([out_re, out_im], axis=0)
    spectra = (
        jnp.transpose(stacked, (3, 1, 0, 2))
        .reshape(chans, feed_dev, 2 * SPECTRA)
        .astype(jnp.bfloat16)
    )
    outgoing = jnp.repeat(spectra, sub, axis=0)
    turned = lax.all_to_all(outgoing, "row", split_axis=0, concat_axis=1, tiled=True)
    turned = turned.reshape(pairs, rows, feed_dev, 2 * SPECTRA)
    gathered = lax.all_gather(turned, "col", axis=2, tiled=True)
    gathered = gathered.reshape(pairs, FEEDS, 2 * SPECTRA)
    pair_index = lax.axis_index("row") * pairs + jnp.arange(pairs)
    starts = pair_index % sub * iblock

    def first_rows(chan_rows, start):
        return lax.dynamic_slice_in_dim(chan_rows, start, iblock, 0)

    left = jax.vmap(first_rows)(gathered, starts)
    second = lax.dynamic_slice_in_dim(gathered, lax.axis_index("col") * jblock, jblock, 1)
    turned_second = jnp.concatenate([-second[:, :, SPECTRA:], second[:, :, :SPECTRA]], axis=2)
    right = jnp.concatenate([second, turned_second], axis=1)
    product = jnp.einsum("pis,pjs->pij", left, right, preferred_element_type=jnp.float32) / SPECTRA
    return product.astype(jnp.bfloat16).reshape(pairs, iblock, 2, jblock)


def shards(voltages, gains):
    rows = lax.axis_size("row")
    cols = lax.axis_size("col")
    fd = voltages.shape[0]
    chans = gains.shape[1]
    if fd % LANES or chans != LANES // 4 or chans % rows or cols != 2 or rows % cols:
        return plain(voltages, gains)
    pairs = chans // rows
    gt = gains.transpose(1, 2, 0).reshape(2 * chans, fd)
    own, other, orders = [], [], []
    first = 0
    for number, share in enumerate(CHUNKS):
        fb = fd * share // sum(CHUNKS)
        final = number + 1 == len(CHUNKS)
        sent = channelize(voltages, gt, first, fb, rows, rows if final else 1)
        sent, gt = lax.optimization_barrier((list(sent), gt))
        first += fb
        if final:
            got = [sent[0]]
            for d in range(1, rows):
                got.append(lax.ppermute(sent[d], "row", [(i, (i + d) % rows) for i in range(rows)]))
            t = jnp.concatenate(got, axis=0)
        else:
            t = lax.all_to_all(sent[0], "row", split_axis=0, concat_axis=0, tiled=True)
        own.append(t)
        other.append(lax.ppermute(t, "col", [(i, (i + 1) % cols) for i in range(cols)]))
        orders.append(final)
    return correlate(own, other, rows, pairs, tuple(orders))


def solution(mesh):
    placed = (P(("band", "row", "col"), None), P(("band", "row", "col"), None, None))
    return jax.shard_map(
        shards,
        mesh=mesh,
        in_specs=placed,
        out_specs=P(("band", "row"), None, None, "col"),
        check_vma=False,
    )
```
